32 devices in a mesh: depth: 4 (over y, x), tile: 8 (over z, core).
Axes of the slice: x: 2, y: 2, z: 4, core: 2. Of those that a mesh axis runs over, the one named last changes fastest.
Arguments:
- objects: float32 [4, 4096, 4096], P('depth', 'tile'), may hold values from -6 to 6
- transfer: bfloat16 [4, 2, 4096, 4096], P('depth', None, None, 'tile'), may hold values from -3 to 3
Outputs:
- sensor: float32 [4096, 4096], P(('depth', 'tile'))
The draws below stay inside these ranges and needn't reach their ends.
All inputs are finite; a program needn't handle non-finite values.
Results may differ from the reference program's by a relative error of at most 0.0003.
Values sent between devices are 32-bit elements; how exact they have to be, the bound alone decides.
A program may use at most 128 MiB of HBM per device.

```python
import jax
import jax.numpy as jnp
from jax import lax

H = 4096
W = 4096
PLANES = 4


def level_of(rng, dims, split, low, largest):
    level, own = 1.0, jax.random.fold_in(rng, 6)
    for axis_at, parts in split:
        steps = jnp.exp(jax.random.uniform(jax.random.fold_in(own, axis_at), (parts,), jnp.float32, low / len(split), largest / len(split)))
        level = level * jnp.repeat(steps, dims[axis_at] // parts).reshape([-1 if axis == axis_at else 1 for axis in range(len(dims))])
    return level


def normal_values(rng, dims, spread, bound, split=(), dtype=jnp.bfloat16):
    values = spread * jax.random.normal(rng, dims, jnp.float32)
    if split:
        values = values * level_of(rng, dims, split, -0.22, 0.18)
    return jnp.clip(values, -bound, bound).astype(dtype)


def setup_inputs(seed: int = 0) -> dict:
    key_list = jax.random.split(jax.random.key(seed), 3)
    objects = normal_values(key_list[0], (PLANES, H, W), 1.0, 6.0, ((0, 4), (1, 8)), jnp.float32)
    transfer = normal_values(key_list[1], (PLANES, 2, H, W), PLANES ** -0.5, 3.0, ((0, 4), (3, 8)))
    return {"objects": objects, "transfer": transfer}


def reference(objects, transfer):
    zeros = jnp.zeros((H, W), jnp.float32)
    start = lax.complex(zeros, zeros)

    def add_plane(summed, items):
        plane_data, response = items
        spectrum = jnp.fft.fft2(plane_data.astype(jnp.float32))
        response = response.astype(jnp.float32)
        return summed + spectrum * lax.complex(response[0], response[1]), None

    weighted, _ = lax.scan(add_plane, start, (objects, transfer))
    return jnp.real(jnp.fft.ifft2(weighted)).astype(jnp.float32)
```

```python
import functools
import math

import jax
import jax.numpy as jnp
import ml_dtypes
import numpy as np
from jax import lax
from jax.experimental import pallas as pl
from jax.experimental.pallas import tpu as pltpu
from jax.sharding import PartitionSpec as P

CHUNKS = 4
STRIP = 16
BF16 = ml_dtypes.bfloat16
F32 = jnp.float32


def halves_np(table):
    table = table.astype(np.float32)
    high = table.astype(BF16)
    low = (table - high.astype(np.float32)).astype(BF16)
    return high, low


def halves(value):
    high = value.astype(jnp.bfloat16)
    return high, (value - high.astype(F32)).astype(jnp.bfloat16)


def angles(rows, cols, modulus):
    turn = (rows[:, None] * cols[None, :]) % modulus
    phase = 2.0 * np.pi * turn / modulus
    return np.cos(phase), np.sin(phase)


def row_matrix(length, groups):
    index = np.arange(length)
    cos, sin = angles(index, index, length)
    width = length // groups
    cos = cos.reshape(length, groups, width)
    sin = sin.reshape(length, groups, width)
    top = np.concatenate([cos, -sin], axis=2).reshape(length, 2 * length)
    bottom = np.concatenate([sin, cos], axis=2).reshape(length, 2 * length)
    return halves_np(np.concatenate([top, bottom], axis=0))


def col_matrix(length):
    index = np.arange(length)
    cos, sin = angles(index, index, length)
    return halves_np(np.block([[cos, sin], [-sin, cos]]))


def dot(left, right):
    return jnp.dot(left, right, preferred_element_type=F32)


def dot3(left_high, left_low, right_high, right_low):
    return dot(left_high, right_high) + (dot(left_high, right_low) + dot(left_low, right_high))


def short_dft(values, sign):
    count = len(values)
    if count == 1:
        return values
    even = short_dft(values[0::2], sign)
    odd = short_dft(values[1::2], sign)
    half = count // 2
    out = [None] * count
    for k in range(half):
        re, im = odd[k]
        if 8 * k == 2 * count:
            re, im = (-sign * im, sign * re)
        elif k:
            c = math.cos(2.0 * math.pi * k / count)
            s = sign * math.sin(2.0 * math.pi * k / count)
            re, im = (re * c - im * s, re * s + im * c)
        out[k] = (even[k][0] + re, even[k][1] + im)
        out[k + half] = (even[k][0] - re, even[k][1] - im)
    return out


def row_kernel(k, x_ref, tw_ref, wh_ref, wl_ref, out_ref, yh, yl):
    rows, full = x_ref.shape
    length = full // CHUNKS
    width = out_ref.shape[-1]

    @pl.when(pl.program_id(0) == 0)
    def _():
        @pl.loop(0, rows // STRIP)
        def _(i):
            at = pl.ds(pl.multiple_of(i * STRIP, STRIP), STRIP)
            for lo in range(0, length, 256):
                x = [x_ref[at, a * length + lo : a * length + lo + 256] for a in range(4)]
                here = slice(lo, lo + 256)
                if k == 0:
                    re = (x[0] + x[2]) + (x[1] + x[3])
                    yh[at, here], yl[at, here] = halves(re)
                else:
                    c, s = (tw_ref[0:1, here], tw_ref[1:2, here])
                    if k == 2:
                        base = (x[0] + x[2]) - (x[1] + x[3])
                        re, im = (base * c, -base * s)
                    else:
                        a, b = (x[0] - x[2], x[1] - x[3])
                        b = -b if k == 1 else b
                        re, im = (a * c + b * s, b * c - a * s)
                    yh[at, here], yl[at, here] = halves(re)
                    there = slice(length + lo, length + lo + 256)
                    yh[at, there], yl[at, there] = halves(im)

    res = dot3(yh[...], yl[...], wh_ref[...], wl_ref[...])
    group = res.shape[1] // 2
    for j in range(group // width):
        for s in range(2):
            out_ref[j, s] = res[:, s * group + j * width : s * group + (j + 1) * width]


def row_chunk(k, x, tw, wh, wl, tiles):
    rows, full = x.shape
    length = full // CHUNKS
    depth = length if k == 0 else 2 * length
    width = length // tiles
    groups, _, double = wh.shape
    part = tiles // groups
    return pl.pallas_call(
        functools.partial(row_kernel, k),
        out_shape=jax.ShapeDtypeStruct((tiles, 2, rows, width), F32),
        grid=(groups,),
        in_specs=[
            pl.BlockSpec((rows, full), lambda t: (0, 0)),
            pl.BlockSpec((2, length), lambda t: (0, 0)),
            pl.BlockSpec((None, depth, double), lambda t: (t, 0, 0)),
            pl.BlockSpec((None, depth, double), lambda t: (t, 0, 0)),
        ],
        out_specs=pl.BlockSpec((part, 2, rows, width), lambda t: (t, 0, 0, 0)),
        scratch_shapes=[pltpu.VMEM((rows, depth), jnp.bfloat16)] * 2,
        compiler_params=pltpu.CompilerParams(vmem_limit_bytes=50 * 2**20),
        cost_estimate=pl.CostEstimate(
            flops=12 * rows * depth * length, bytes_accessed=rows * full * 8, transcendentals=0
        ),
        name=f"row{k}",
    )(x, tw, wh, wl)


def col_kernel(d_ref, t_ref, tw_ref, mh_ref, ml_ref, out_ref, yh, yl, ph, plow, res_ref):
    tiles, _, rows, width = d_ref.shape
    pitch = yh.shape[1] // tiles
    block = out_ref.shape[2]

    @pl.loop(0, rows // STRIP)
    def _(i):
        at = pl.ds(pl.multiple_of(i * STRIP, STRIP), STRIP)
        below = pl.ds(pl.multiple_of(rows + i * STRIP, STRIP), STRIP)
        out = short_dft([(d_ref[a, 0, at, :], d_ref[a, 1, at, :]) for a in range(tiles)], -1.0)
        for kk in range(tiles):
            re, im = out[kk]
            if kk:
                c, s = (tw_ref[kk, 0, at, :], tw_ref[kk, 1, at, :])
                re, im = (re * c + im * s, im * c - re * s)
            lanes = slice(kk * pitch, kk * pitch + width)
            yh[at, lanes], yl[at, lanes] = halves(re)
            yh[below, lanes], yl[below, lanes] = halves(im)

    @pl.loop(0, tiles // 2)
    def _(g):
        lanes = pl.ds(pl.multiple_of(g * 2 * pitch, 2 * pitch), 2 * pitch)
        spec = dot3(mh_ref[...], ml_ref[...], yh[:, lanes], yl[:, lanes])
        for h in range(2):
            there = slice(h * pitch, h * pitch + width)
            re, im = (spec[:rows, there], spec[rows:, there])
            tr = t_ref[0, 2 * g + h].astype(F32)
            ti = t_ref[1, 2 * g + h].astype(F32)
            ph[:rows, there], plow[:rows, there] = halves(re * ti + im * tr)
            ph[rows:, there], plow[rows:, there] = halves(re * tr - im * ti)
        back = dot3(mh_ref[...], ml_ref[...], ph[...], plow[...])
        for h in range(2):
            res_ref[2 * g + h] = back[:, h * pitch : h * pitch + width]

    @pl.loop(0, rows // STRIP)
    def _(i):
        at = pl.ds(pl.multiple_of(i * STRIP, STRIP), STRIP)
        below = pl.ds(pl.multiple_of(rows + i * STRIP, STRIP), STRIP)
        parts = []
        for kk in range(tiles):
            re, im = (res_ref[kk, below, :], res_ref[kk, at, :])
            if kk:
                c, s = (tw_ref[kk, 0, at, :], tw_ref[kk, 1, at, :])
                re, im = (re * c - im * s, im * c + re * s)
            parts.append((re, im))
        out = short_dft(parts, 1.0)
        for a in range(tiles):
            for s in range(2):
                if block >= STRIP:
                    per = block // STRIP
                    spot = pl.ds(pl.multiple_of((i % per) * STRIP, STRIP), STRIP)
                    out_ref[a * (rows // block) + i // per, s, spot, :] = out[a][s]
                else:
                    per = STRIP // block
                    for b in range(per):
                        piece = out[a][s][b * block : (b + 1) * block]
                        out_ref[a * (rows // block) + i * per + b, s] = piece


def col_chunk(k, data, response, tw, mh, ml, block):
    tiles, _, rows, width = data.shape
    pitch = max(width, 128)
    vm = pl.BlockSpec(memory_space=pltpu.VMEM)
    return pl.pallas_call(
        col_kernel,
        out_shape=jax.ShapeDtypeStruct((tiles * rows // block, 2, block, width), F32),
        in_specs=[vm] * 5,
        out_specs=vm,
        scratch_shapes=[pltpu.VMEM((2 * rows, tiles * pitch), jnp.bfloat16)] * 2
        + [pltpu.VMEM((2 * rows, 2 * pitch), jnp.bfloat16)] * 2
        + [pltpu.VMEM((tiles, 2 * rows, width), F32)],
        compiler_params=pltpu.CompilerParams(vmem_limit_bytes=56 * 2**20),
        cost_estimate=pl.CostEstimate(
            flops=48 * rows * rows * tiles * width,
            bytes_accessed=tiles * rows * width * 24,
            transcendentals=0,
        ),
        name=f"col{k}",
    )(data, response, tw, mh, ml)


def last_kernel(k, e_ref, tw_ref, wh_ref, wl_ref, *rest):
    acc_ref = rest[0] if k else None
    out_ref, yh, yl = rest[-3:]
    tiles, _, rows, width = e_ref.shape
    length = tiles * width
    group = wh_ref.shape[-1] // 2

    @pl.when(pl.program_id(0) == 0)
    def _():
        for t in range(tiles):
            for s in range(2):
                lo = (1 - s) * length + t * width
                yh[:, lo : lo + width], yl[:, lo : lo + width] = halves(e_ref[t, s])

    res = dot3(yh[...], yl[...], wh_ref[...], wl_ref[...])
    im, re = (res[:, :group], res[:, group:])
    c, s = (tw_ref[0:1, :], tw_ref[1:2, :])
    if k == 0:
        real = re * c
        terms = [real] * 4
    else:
        real, imag = (re * c - im * s, re * s + im * c)
        turns = [real, -imag, -real, imag]
        terms = [turns[(k * a) % 4] for a in range(4)]
    for a in range(4):
        spot = pl.ds(pl.multiple_of(a * length + pl.program_id(0) * group, group), group)
        out_ref[:, spot] = terms[a] if k == 0 else acc_ref[:, spot] + terms[a]


def last_chunk(k, data, tw, wh, wl, acc):
    tiles, _, rows, width = data.shape
    length = tiles * width
    groups, _, double = wh.shape
    specs = [
        pl.BlockSpec((tiles, 2, rows, width), lambda t: (0, 0, 0, 0)),
        pl.BlockSpec((2, double // 2), lambda t: (0, t)),
        pl.BlockSpec((None, 2 * length, double), lambda t: (t, 0, 0)),
        pl.BlockSpec((None, 2 * length, double), lambda t: (t, 0, 0)),
    ]
    part = pl.BlockSpec((rows, 4 * length), lambda t: (0, 0))
    args = [data, tw, wh, wl]
    if k:
        specs.append(part)
        args.append(acc)
    return pl.pallas_call(
        functools.partial(last_kernel, k),
        out_shape=jax.ShapeDtypeStruct((rows, 4 * length), F32),
        grid=(groups,),
        in_specs=specs,
        out_specs=part,
        scratch_shapes=[pltpu.VMEM((rows, 2 * length), jnp.bfloat16)] * 2,
        compiler_params=pltpu.CompilerParams(vmem_limit_bytes=40 * 2**20),
        cost_estimate=pl.CostEstimate(
            flops=24 * rows * length * length, bytes_accessed=2**24, transcendentals=0
        ),
        name=f"last{k}",
    )(*args)


def body(objects, transfer):
    tiles = lax.axis_size("tile")
    depths = lax.axis_size("depth")
    rows, full = objects.shape[1:]
    height = rows * tiles
    length = full // CHUNKS
    width = length // tiles
    block = height // (tiles * depths)
    group = max(width, 128)
    groups = length // group
    wh, wl = (
        jnp.asarray(
            np.ascontiguousarray(
                table.reshape(2 * length, groups, 2 * group).transpose(1, 0, 2)
            )
        )
        for table in row_matrix(length, groups)
    )
    mh, ml = (jnp.asarray(m) for m in col_matrix(rows))
    twist = np.stack(angles(np.arange(CHUNKS), np.arange(length), full), axis=1).astype(np.float32)
    final = jnp.asarray(twist / (height * full))
    twist = jnp.asarray(twist)
    turn = np.stack(angles(np.arange(tiles), np.arange(rows), height), axis=1).astype(np.float32)
    turn = jnp.broadcast_to(jnp.asarray(turn)[..., None], turn.shape + (width,))

    pick = np.zeros((CHUNKS * width, CHUNKS, width), np.float32)
    for k in range(CHUNKS):
        for m in range(width):
            pick[CHUNKS * m + k, k, m] = 1.0
    pick = jnp.asarray(pick.astype(BF16))
    split = transfer[0].reshape(2, rows, tiles, CHUNKS * width)
    response = [
        jnp.einsum("smkl,lw->skmw", split, pick[:, k], preferred_element_type=F32).astype(
            jnp.bfloat16
        )
        for k in range(CHUNKS)
    ]

    x = objects[0]
    sent = [row_chunk(k, x, twist[k], wh, wl, tiles) for k in range(CHUNKS)]
    acc = None
    for k in range(CHUNKS):
        bands = lax.all_to_all(sent[k], "tile", split_axis=0, concat_axis=0, tiled=True)
        back = col_chunk(k, bands, response[k], turn, mh, ml, block)
        summed = lax.psum_scatter(back, "depth", scatter_dimension=0, tiled=True)
        owned = lax.all_to_all(summed, "tile", split_axis=0, concat_axis=0, tiled=True)
        acc = last_chunk(k, owned, final[k], wh, wl, acc)
    return acc


def solution(mesh):
    in_specs = (P("depth", "tile", None), P("depth", None, None, "tile"))
    out_specs = P(("depth", "tile"), None)
    return jax.shard_map(body, mesh=mesh, in_specs=in_specs, out_specs=out_specs, check_vma=False)
```
